32 devices in a mesh: comp: 16 (over z, x, core), rows: 2 (over y).
Axes of the slice: x: 2, y: 2, z: 4, core: 2. Of those that a mesh axis runs over, the one named last changes fastest.
Arguments:
- hidden_states: bfloat16 [2, 2, 16, 128, 2560], P('rows', None, 'comp'), may hold values from -6 to 6
- queries: bfloat16 [2, 2, 16, 128, 1280], P('rows', None, 'comp'), may hold values from -900 to 900
- new_keys: bfloat16 [2, 2, 16, 128, 1280], P('rows', None, 'comp'), may hold values from -6 to 6
- new_values: bfloat16 [2, 2, 16, 128, 1280], P('rows', None, 'comp'), may hold values from -6 to 6
- out_grad: bfloat16 [2, 2, 16, 128, 1280], P('rows', None, 'comp'), may hold values from -6 to 6
- gate_weight: bfloat16 [2560, 128], replicated, may hold values from -0.125 to 0.125
- gate_bias: float32 [128], replicated, may hold values from -2 to 6
- prompt_state: float32 [2, 16, 2, 2, 2, 64, 640], P('rows', 'comp'), may hold values from -6 to 6
- owners: int32 [2, 2], P('rows'), may hold values from 0 to 15
- lengths: int32 [2, 2, 16], P('rows', None, 'comp'), may hold values from 32 to 128
- advantage: float32 [2, 2, 16], P('rows', None, 'comp'), may hold values from -4 to 4
Outputs:
- d_queries: bfloat16 [2, 2, 16, 128, 1280], P('rows', None, 'comp')
- d_keys: bfloat16 [2, 2, 16, 128, 1280], P('rows', None, 'comp')
- d_values: bfloat16 [2, 2, 16, 128, 1280], P('rows', None, 'comp')
- d_hidden: bfloat16 [2, 2, 16, 128, 2560], P('rows', None, 'comp')
- d_gate_weight: float32 [2560, 128], replicated
- d_gate_bias: float32 [128], replicated
- d_state: float32 [2, 2, 2, 2, 64, 640], P('rows', None, None, None, 'comp')
The draws below stay inside these ranges and needn't reach their ends.
All inputs are finite; a program needn't handle non-finite values.
Results may differ from the reference program's by a relative error of at most 0.011.
Values sent between devices are 32-bit elements; how exact they have to be, the bound alone decides.
A program may use at most 64 MiB of HBM per device.

```python
import jax
import jax.numpy as jnp
from jax import lax

D = 2560
H = 2
DH = 640
M = 64
LEN = 128
PR_ROW = 2
COMPS = 16
N_COMP = 16
N_ROWS = 2


def draw_queries(key, part):
    shape = (N_ROWS, PR_ROW, COMPS, LEN, H * DH)
    values = jnp.clip(jax.random.normal(key, shape, jnp.float32), -6.0, 6.0)
    return values.astype(jnp.bfloat16)


def plant(drawn, rng, low, largest):
    spot = [jax.random.randint(jax.random.fold_in(rng, axis), (), 0, length) for axis, length in enumerate(drawn.shape)]
    main_axis = drawn.shape.index(max(drawn.shape))
    beside = spot[:main_axis] + [(spot[main_axis] + 1) % drawn.shape[main_axis]] + spot[main_axis + 1:]
    return drawn.at[tuple(spot)].set(low).at[tuple(beside)].set(largest)


def block_levels(own_key, dims, pieces, low, largest):
    level, own = 1.0, jax.random.fold_in(own_key, 6)
    for dim, blocks in pieces:
        draws = jnp.exp(jax.random.uniform(jax.random.fold_in(own, dim), (blocks,), jnp.float32, low / len(pieces), largest / len(pieces)))
        level = level * jnp.repeat(draws, dims[dim] // blocks).reshape([-1 if axis == dim else 1 for axis in range(len(dims))])
    return level


def noise(rng, extent, scale, limit, split=(), kind=jnp.bfloat16):
    array = scale * jax.random.normal(rng, extent, jnp.float32)
    if split:
        array = array * block_levels(rng, extent, split, -0.22, 0.18)
    return jnp.clip(array, -limit, limit).astype(kind)


def setup_inputs(seed: int = 0) -> dict:
    arg_keys = jax.random.split(jax.random.key(seed), 12)
    hidden_states = noise(arg_keys[0], (N_ROWS, PR_ROW, COMPS, LEN, D), 1.0, 6.0, ((0, 2), (2, 16)))
    queries = draw_queries(jax.random.fold_in(arg_keys[11], 71), 0)
    new_keys = noise(arg_keys[2], (N_ROWS, PR_ROW, COMPS, LEN, H * DH), 1.0, 6.0, ((0, 2), (2, 16)))
    new_values = noise(arg_keys[3], (N_ROWS, PR_ROW, COMPS, LEN, H * DH), 1.0, 6.0, ((0, 2), (2, 16)))
    out_grad = noise(arg_keys[4], (N_ROWS, PR_ROW, COMPS, LEN, H * DH), 1.0, 6.0, ((0, 2), (2, 16)))
    gate_weight = noise(arg_keys[5], (D, H * M), D ** -0.5, 0.125)
    gate_bias = jnp.clip(jax.random.uniform(arg_keys[6], (H * M,), jnp.float32, -2.0, 6.0), -2.0, 6.0)
    prompt_state = noise(arg_keys[7], (N_ROWS, N_COMP, PR_ROW, 2, H, M, DH), 1.0, 6.0, ((0, 2), (1, 16)), jnp.float32)
    owners = plant(jax.random.randint(arg_keys[8], (N_ROWS, PR_ROW), 0, N_COMP), jax.random.fold_in(arg_keys[8], 1), 0, N_COMP - 1).astype(jnp.int32)
    lengths = plant(jax.random.randint(arg_keys[9], (N_ROWS, PR_ROW, COMPS), LEN // 4, LEN + 1), jax.random.fold_in(arg_keys[9], 1), LEN // 4, LEN).astype(jnp.int32)
    advantage = noise(arg_keys[10], (N_ROWS, PR_ROW, COMPS), 1.0, 4.0, ((0, 2), (2, 16)), jnp.float32)
    return {"hidden_states": hidden_states, "queries": queries, "new_keys": new_keys, "new_values": new_values, "out_grad": out_grad, "gate_weight": gate_weight, "gate_bias": gate_bias, "prompt_state": prompt_state, "owners": owners, "lengths": lengths, "advantage": advantage}


def slot_forward(gates, queries, keys_in, values_in, anchor_point):
    steps = queries.shape[0]
    heads = anchor_point.shape[1]
    slots = anchor_point.shape[2]
    width = anchor_point.shape[3]
    highest_score = lax.Precision.HIGHEST
    log_keep = jax.nn.log_sigmoid(gates).reshape(steps, heads, slots) / 8.0
    running = jnp.cumsum(log_keep, axis=0)
    inflow = -jnp.expm1(log_keep)
    places = jnp.arange(steps, dtype=jnp.int32)
    lower = (places[:, None] >= places[None, :])[:, :, None, None]
    between = running[:, None] - running[None, :]
    reach = jnp.where(lower, jnp.exp(jnp.where(lower, between, 0.0)), 0.0) * inflow[None]
    score_scale = width ** (-0.5)
    query_head_count = queries.astype(jnp.float32).reshape(steps, heads, width)
    key_heads = keys_in.astype(jnp.float32).reshape(steps, heads, width)
    value_heads = values_in.astype(jnp.float32).reshape(steps, heads, width)
    pairs = jnp.einsum('thd,jhd->thj', query_head_count, key_heads) * score_scale
    carried_state = jnp.exp(running)
    anchor_score_rows = jnp.einsum('icv,crv->icr', query_head_count, anchor_point[0], precision=highest_score) * score_scale
    scores = jnp.einsum('tjhm,thj->thm', reach, pairs, precision=highest_score) + carried_state * anchor_score_rows
    slot_probabilities = jax.nn.softmax(scores, axis=-1)
    mixing = jnp.einsum('thm,tjhm->thj', slot_probabilities, reach, precision=highest_score).astype(jnp.bfloat16)
    result_output = jnp.einsum('thj,jhd->thd', mixing.astype(jnp.float32), value_heads)
    result_output = result_output + jnp.einsum('ivw,vwb->ivb', slot_probabilities * carried_state, anchor_point[1], precision=highest_score)
    return result_output.reshape(steps, heads * width)

def completion_grads(tokens, queries, keys_in, values_in, out_grad, gate_weight, gate_bias, anchor_point, length, advantage):
    steps = queries.shape[0]
    gates = jnp.dot(tokens, gate_weight, preferred_element_type=jnp.float32) + gate_bias
    places = jnp.arange(steps, dtype=jnp.int32)
    live = jnp.where(places < length, 1.0, 0.0).astype(jnp.float32)
    cotangent = (advantage * live)[:, None] * out_grad.astype(jnp.float32)
    result_output, pullback = jax.vjp(slot_forward, gates, queries, keys_in, values_in, anchor_point)
    grad_gates, grad_q, grad_k, grad_v, grad_anchor = pullback(cotangent)
    gates_low = grad_gates.astype(jnp.bfloat16)
    grad_tokens = jnp.dot(gates_low, gate_weight.T, preferred_element_type=jnp.float32).astype(jnp.bfloat16)
    grad_weight = jnp.dot(tokens.T, gates_low, preferred_element_type=jnp.float32)
    grad_bias = lax.optimization_barrier(jnp.sum(grad_gates, axis=0))
    return (grad_q.astype(jnp.bfloat16), grad_k.astype(jnp.bfloat16), grad_v.astype(jnp.bfloat16), grad_tokens, grad_weight, grad_bias, grad_anchor)

def reference(hidden_states, queries, new_keys, new_values, out_grad, gate_weight, gate_bias, prompt_state, owners, lengths, advantage):
    total = N_ROWS * PR_ROW * COMPS

    def visit(carry, index):
        sum_weight, sum_bias, sum_state = carry
        row = index // (PR_ROW * COMPS)
        prompt = index // COMPS % PR_ROW
        column = index % COMPS
        anchor_point = prompt_state[row, owners[row, prompt], prompt]
        grads = completion_grads(hidden_states[row, prompt, column], queries[row, prompt, column], new_keys[row, prompt, column], new_values[row, prompt, column], out_grad[row, prompt, column], gate_weight, gate_bias, anchor_point, lengths[row, prompt, column], advantage[row, prompt, column])
        sum_state = sum_state.at[row, prompt].add(grads[6])
        return ((sum_weight + grads[4], sum_bias + grads[5], sum_state), (grads[0], grads[1], grads[2], grads[3]))
    start = (jnp.zeros((D, H * M), jnp.float32), jnp.zeros((H * M,), jnp.float32), jnp.zeros((N_ROWS, PR_ROW, 2, H, M, DH), jnp.float32))
    (sum_weight, sum_bias, sum_state), stacked = lax.scan(visit, start, jnp.arange(total, dtype=jnp.int32))
    shape_heads = (N_ROWS, PR_ROW, COMPS, LEN, H * DH)
    d_queries = stacked[0].reshape(shape_heads)
    d_keys = stacked[1].reshape(shape_heads)
    d_values = stacked[2].reshape(shape_heads)
    d_hidden = stacked[3].reshape((N_ROWS, PR_ROW, COMPS, LEN, D))
    return (d_queries, d_keys, d_values, d_hidden, sum_weight, sum_bias, sum_state)
```

```python
import functools

import jax
import jax.numpy as jnp
from jax import lax
from jax.experimental import pallas as pl
from jax.experimental.pallas import tpu as pltpu
from jax.sharding import PartitionSpec as P

F32 = jnp.float32
BF16 = jnp.bfloat16
NN = (((1,), (0,)), ((), ()))
NT = (((1,), (1,)), ((), ()))
TN = (((0,), (0,)), ((), ()))


def dot(a, b, dims=NN):
    return lax.dot_general(a, b, dims, preferred_element_type=F32)


def dot_full(a, b, dims=NN):
    return lax.dot_general(
        a, b, dims, precision=lax.Precision.HIGHEST, preferred_element_type=F32
    )


def pieces(x, count):
    out = []
    for _ in range(count):
        top = x.astype(BF16)
        out.append(top)
        x = x - top.astype(F32)
    return out


def mix_kernel(
    lengths_ref, advantage_ref, x_ref, q_ref, k_ref, v_ref, og_ref, w_ref, bias_ref, anchor_ref,
    dq_ref, dk_ref, dv_ref, dx_ref, dw_ref, db_ref, ds_ref,
    decay_ref, flow_ref, mix_ref, pair_ref, *, chunk,
):
    prompt = pl.program_id(0)
    steps = x_ref.shape[1]
    heads, slots, width = anchor_ref.shape[2:]
    lanes = heads * slots
    blocks = steps // chunk
    scale = width ** (-0.5)
    lane = lax.broadcasted_iota(jnp.int32, (1, lanes), 1)
    of_head = [(lane >= h * slots) & (lane < (h + 1) * slots) for h in range(heads)]
    row = lax.broadcasted_iota(jnp.int32, (steps, 1), 0)
    column = lax.broadcasted_iota(jnp.int32, (1, steps), 1)
    local = lax.broadcasted_iota(jnp.int32, (chunk, 1), 0)
    lower = jnp.where(row >= column, 1.0, 0.0).astype(BF16)

    def by_head(parts):
        out = parts[-1]
        for h in range(heads - 2, -1, -1):
            out = jnp.where(lane < (h + 1) * slots, parts[h], out)
        return out

    def head_reduce(x, op):
        return by_head(
            [op(x[:, h * slots:(h + 1) * slots], axis=1, keepdims=True) for h in range(heads)]
        )

    def head(ref, h):
        return ref[0, :, h * width:(h + 1) * width]

    x = x_ref[0]
    w = w_ref[...]
    gates = dot(x, w) + bias_ref[...]
    small = jnp.exp(-jnp.abs(gates))
    one = 1.0 + small
    gap = one - 1.0
    log_one = jnp.where(gap == 0.0, small, jnp.log(one) * (small / jnp.where(gap == 0.0, 1.0, gap)))
    keep = -(jnp.maximum(-gates, 0.0) + log_one) / 8.0
    down = jnp.where(gates >= 0.0, small, 1.0) / one
    kept = jnp.exp(keep)
    series = jnp.ones_like(keep)
    for degree in range(9, 1, -1):
        series = 1.0 + keep * series * (1.0 / degree)
    inflow = jnp.where(keep > -0.5, -keep * series, 1.0 - kept)
    cum = sum(dot(lower, part) for part in pieces(keep, 3))
    carried = jnp.exp(cum)

    live = jnp.where(row < lengths_ref[prompt], advantage_ref[prompt], 0.0)
    qk, dm, seen, back = [], [], [], []
    for h in range(heads):
        q, og = head(q_ref, h), head(og_ref, h)
        qk.append(dot(q, head(k_ref, h), NT) * scale)
        dm.append(dot(og, head(v_ref, h), NT) * live)
        seen.append(sum(dot(q, part, NT) for part in pieces(anchor_ref[0, 0, h], 3)))
        back.append(sum(dot(og, part, NT) for part in pieces(anchor_ref[0, 1, h], 3)))
    seen = jnp.concatenate(seen, axis=1) * (scale * carried)
    back = jnp.concatenate(back, axis=1) * (live * carried)

    def block_rows(b):
        rows = slice(b * chunk, (b + 1) * chunk)
        return jnp.concatenate([part for h in range(heads) for part in (qk[h][rows], dm[h][rows])])

    def before(b):
        start = cum[b * chunk - 1:b * chunk]
        far = jnp.where(row < b * chunk, jnp.exp(start - cum), 0.0)
        near = jnp.exp(cum[b * chunk:(b + 1) * chunk] - start)
        return far, near

    def columns(parts, rows, at):
        return by_head([part[rows, at:at + 1] for part in parts])

    scores, d_probs = [], []
    for b in range(blocks):
        rows = slice(b * chunk, (b + 1) * chunk)
        score, d_prob = seen[rows], back[rows]
        for j in range(chunk):
            at = b * chunk + j
            decay = jnp.where(local >= j, jnp.exp(cum[rows] - cum[at:at + 1]), 0.0)
            decay_ref[at] = decay
            reach = decay * inflow[at:at + 1]
            score = score + reach * columns(qk, rows, at)
            d_prob = d_prob + reach * columns(dm, rows, at)
        if b:
            far, near = before(b)
            got = dot_full(block_rows(b), far * inflow)
            got = [got[i * chunk:(i + 1) * chunk] for i in range(2 * heads)]
            score = score + near * by_head(got[0::2])
            d_prob = d_prob + near * by_head(got[1::2])
        scores.append(score)
        d_probs.append(d_prob)
    scores = jnp.concatenate(scores)
    d_probs = jnp.concatenate(d_probs)
    probs = jnp.exp(scores - head_reduce(scores, jnp.max))
    probs = probs / head_reduce(probs, jnp.sum)
    weighted = probs * d_probs
    d_scores = probs * (d_probs - head_reduce(weighted, jnp.sum))

    flow_ref[...] = jnp.zeros_like(flow_ref)
    for b in range(blocks):
        rows = slice(b * chunk, (b + 1) * chunk)
        mix = [jnp.zeros((chunk, steps), F32)] * heads
        pair = [jnp.zeros((chunk, steps), F32)] * heads
        if b:
            far, near = before(b)
            left = [probs[rows] * near, d_scores[rows] * near]
            left = jnp.concatenate(
                [jnp.where(mine, part, 0.0) for mine in of_head for part in (left[1], left[0])]
            )
            got = dot_full(left, far * inflow, NT)
            for h in range(heads):
                pair[h] = got[2 * h * chunk:(2 * h + 1) * chunk]
                mix[h] = got[(2 * h + 1) * chunk:(2 * h + 2) * chunk]
            flow_ref[...] += far * dot_full(block_rows(b), left, TN)
        for j in range(chunk):
            at = b * chunk + j
            decay = decay_ref[at]
            up, down_part = decay * probs[rows], decay * d_scores[rows]
            flow_ref[at:at + 1] += jnp.sum(
                up * columns(dm, rows, at) + down_part * columns(qk, rows, at),
                axis=0, keepdims=True,
            )
            up, down_part = up * inflow[at:at + 1], down_part * inflow[at:at + 1]
            for h in range(heads):
                part = slice(h * slots, (h + 1) * slots)
                here = column == at
                mix[h] = jnp.where(here, jnp.sum(up[:, part], axis=1, keepdims=True), mix[h])
                pair[h] = jnp.where(
                    here, jnp.sum(down_part[:, part], axis=1, keepdims=True), pair[h]
                )
        for h in range(heads):
            mix_ref[h, rows] = mix[h]
            pair_ref[h, rows] = pair[h]

    from_scores = d_scores * carried * scale
    from_probs = probs * carried * live
    for h in range(heads):
        part = slice(h * slots, (h + 1) * slots)
        at = slice(h * width, (h + 1) * width)
        q, og = head(q_ref, h), head(og_ref, h)
        pair = (pair_ref[h] * scale).astype(BF16)
        state_high, state_low = pieces(from_scores[:, part], 2)
        key_high, key_low = pieces(anchor_ref[0, 0, h], 2)
        d_q = dot(pair, head(k_ref, h)) + dot(state_high, key_high)
        d_q = d_q + dot(state_high, key_low) + dot(state_low, key_high)
        dq_ref[0, :, at] = d_q.astype(BF16)
        dk_ref[0, :, at] = dot(pair, q, TN).astype(BF16)
        cotangent = (og.astype(F32) * live).astype(BF16)
        dv_ref[0, :, at] = dot(mix_ref[h].astype(BF16), cotangent, TN).astype(BF16)
        ds_ref[0, 0, h] = dot(state_high, q, TN) + dot(state_low, q, TN)
        high, low = pieces(from_probs[:, part], 2)
        ds_ref[0, 1, h] = dot(high, og, TN) + dot(low, og, TN)

    flow = flow_ref[...]
    d_cum = weighted + d_scores * scores - flow * inflow
    d_keep = sum(dot(lower, part, TN) for part in pieces(d_cum, 3)) - flow * kept
    d_gates = d_keep * down * 0.125
    low = d_gates.astype(BF16)
    dx_ref[0] = dot(low, w, NT).astype(BF16)
    d_w = dot(x, low, TN)
    d_b = jnp.sum(d_gates, axis=0, keepdims=True)

    @pl.when(prompt == 0)
    def _():
        dw_ref[...] = d_w
        db_ref[...] = d_b

    @pl.when(prompt > 0)
    def _():
        dw_ref[...] += d_w
        db_ref[...] += d_b


def local_grads(x, q, k, v, og, weight, bias, anchors, lengths, advantage, interpret=False):
    prompts, steps, depth = x.shape
    inner = q.shape[2]
    lanes = weight.shape[1]
    heads = anchors.shape[2]
    chunk = 16

    def per_prompt(a):
        shape = (1,) + a.shape[1:]
        return pl.BlockSpec(shape, lambda p: (p,) + (0,) * (len(shape) - 1))

    def whole(shape):
        return pl.BlockSpec(shape, lambda p: (0,) * len(shape))

    smem = pl.BlockSpec(memory_space=pltpu.SMEM)
    shapes = (
        jax.ShapeDtypeStruct(q.shape, BF16),
        jax.ShapeDtypeStruct(q.shape, BF16),
        jax.ShapeDtypeStruct(q.shape, BF16),
        jax.ShapeDtypeStruct(x.shape, BF16),
        jax.ShapeDtypeStruct(weight.shape, F32),
        jax.ShapeDtypeStruct((1, lanes), F32),
        jax.ShapeDtypeStruct(anchors.shape, F32),
    )
    return pl.pallas_call(
        functools.partial(mix_kernel, chunk=chunk),
        grid=(prompts,),
        out_shape=shapes,
        in_specs=[smem, smem] + [per_prompt(a) for a in (x, q, k, v, og)]
        + [whole(weight.shape), whole((1, lanes)), per_prompt(anchors)],
        out_specs=tuple(per_prompt(s) for s in shapes[:4])
        + (whole(weight.shape), whole((1, lanes)), per_prompt(anchors)),
        scratch_shapes=[
            pltpu.VMEM((steps, chunk, lanes), F32),
            pltpu.VMEM((steps, lanes), F32),
            pltpu.VMEM((heads, steps, steps), F32),
            pltpu.VMEM((heads, steps, steps), F32),
        ],
        compiler_params=pltpu.CompilerParams(
            dimension_semantics=("arbitrary",), vmem_limit_bytes=48 * 2**20
        ),
        interpret=interpret,
    )(lengths, advantage, x, q, k, v, og, weight, bias.reshape(1, lanes), anchors)


def shards(
    hidden_states, queries, new_keys, new_values, out_grad, gate_weight, gate_bias,
    prompt_state, owners, lengths, advantage,
):
    me = lax.axis_index("comp")
    mine = (owners[0] == me)[:, None, None, None, None]
    anchors = lax.psum(jnp.where(mine, prompt_state[0, 0], 0.0), "comp")
    dq, dk, dv, dx, d_weight, d_bias, d_state = local_grads(
        hidden_states[0, :, 0], queries[0, :, 0], new_keys[0, :, 0], new_values[0, :, 0],
        out_grad[0, :, 0], gate_weight, gate_bias, anchors, lengths[0, :, 0], advantage[0, :, 0],
    )
    d_state = lax.psum_scatter(d_state, "comp", scatter_dimension=3, tiled=True)
    block = lax.psum_scatter(d_weight, "comp", scatter_dimension=0, tiled=True)
    block = lax.psum(block, "rows")
    d_weight = lax.all_gather(block, "comp", axis=0, tiled=True)
    d_bias = lax.psum(d_bias, ("comp", "rows"))[0]
    return (
        dq[None, :, None], dk[None, :, None], dv[None, :, None], dx[None, :, None],
        d_weight, d_bias, d_state[None],
    )


def solution(mesh):
    tokens = P("rows", None, "comp", None, None)
    return jax.shard_map(
        shards,
        mesh=mesh,
        in_specs=(
            tokens, tokens, tokens, tokens, tokens, P(), P(),
            P("rows", "comp", None, None, None, None, None),
            P("rows", None), P("rows", None, "comp"), P("rows", None, "comp"),
        ),
        out_specs=(
            tokens, tokens, tokens, tokens, P(), P(),
            P("rows", None, None, None, "comp", None),
        ),
        check_vma=False,
    )
```

```python
import functools

import jax
import jax.numpy as jnp
from jax import lax
from jax.experimental import pallas as pl
from jax.experimental.pallas import tpu as pltpu
from jax.sharding import PartitionSpec as P

F32 = jnp.float32
BF16 = jnp.bfloat16
NN = (((1,), (0,)), ((), ()))
NT = (((1,), (1,)), ((), ()))
TN = (((0,), (0,)), ((), ()))


def dot(a, b, dims=NN):
    return lax.dot_general(a, b, dims, preferred_element_type=F32)


def dot_full(a, b, dims=NN):
    return lax.dot_general(
        a, b, dims, precision=lax.Precision.HIGHEST, preferred_element_type=F32
    )


def pieces(x, count):
    out = []
    for _ in range(count):
        top = x.astype(BF16)
        out.append(top)
        x = x - top.astype(F32)
    return out


def mix_kernel(
    lengths_ref, advantage_ref, x_ref, q_ref, k_ref, v_ref, og_ref, w_ref, bias_ref, anchor_ref,
    dq_ref, dk_ref, dv_ref, dx_ref, dw_ref, db_ref, ds_ref,
    decay_ref, flow_ref, mix_ref, pair_ref, *, chunk,
):
    prompt = pl.program_id(0)
    steps = x_ref.shape[1]
    heads, slots, width = anchor_ref.shape[2:]
    lanes = heads * slots
    blocks = steps // chunk
    scale = width ** (-0.5)
    lane = lax.broadcasted_iota(jnp.int32, (1, lanes), 1)
    of_head = [(lane >= h * slots) & (lane < (h + 1) * slots) for h in range(heads)]
    row = lax.broadcasted_iota(jnp.int32, (steps, 1), 0)
    column = lax.broadcasted_iota(jnp.int32, (1, steps), 1)
    local = lax.broadcasted_iota(jnp.int32, (chunk, 1), 0)
    lower = jnp.where(row >= column, 1.0, 0.0).astype(BF16)

    def by_head(parts):
        out = parts[-1]
        for h in range(heads - 2, -1, -1):
            out = jnp.where(lane < (h + 1) * slots, parts[h], out)
        return out

    def head_reduce(x, op):
        return by_head(
            [op(x[:, h * slots:(h + 1) * slots], axis=1, keepdims=True) for h in range(heads)]
        )

    def head(ref, h):
        return ref[0, :, h * width:(h + 1) * width]

    x = x_ref[0]
    w = w_ref[...]
    gates = dot(x, w) + bias_ref[...]
    small = jnp.exp(-jnp.abs(gates))
    one = 1.0 + small
    gap = one - 1.0
    log_one = jnp.where(gap == 0.0, small, jnp.log(one) * (small / jnp.where(gap == 0.0, 1.0, gap)))
    keep = -(jnp.maximum(-gates, 0.0) + log_one) / 8.0
    down = jnp.where(gates >= 0.0, small, 1.0) / one
    kept = jnp.exp(keep)
    series = jnp.ones_like(keep)
    for degree in range(9, 1, -1):
        series = 1.0 + keep * series * (1.0 / degree)
    inflow = jnp.where(keep > -0.5, -keep * series, 1.0 - kept)
    cum = sum(dot(lower, part) for part in pieces(keep, 3))
    carried = jnp.exp(cum)

    live = jnp.where(row < lengths_ref[prompt], advantage_ref[prompt], 0.0)
    qk, dm, seen, back = [], [], [], []
    for h in range(heads):
        q, og = head(q_ref, h), head(og_ref, h)
        qk.append(dot(q, head(k_ref, h), NT) * scale)
        dm.append(dot(og, head(v_ref, h), NT) * live)
        seen.append(sum(dot(q, part, NT) for part in pieces(anchor_ref[0, 0, h], 3)))
        back.append(sum(dot(og, part, NT) for part in pieces(anchor_ref[0, 1, h], 3)))
    seen = jnp.concatenate(seen, axis=1) * (scale * carried)
    back = jnp.concatenate(back, axis=1) * (live * carried)

    def block_rows(b):
        rows = slice(b * chunk, (b + 1) * chunk)
        return jnp.concatenate([part for h in range(heads) for part in (qk[h][rows], dm[h][rows])])

    def before(b):
        start = cum[b * chunk - 1:b * chunk]
        far = jnp.where(row < b * chunk, jnp.exp(start - cum), 0.0)
        near = jnp.exp(cum[b * chunk:(b + 1) * chunk] - start)
        return far, near

    def columns(parts, rows, at):
        return by_head([part[rows, at:at + 1] for part in parts])

    scores, d_probs = [], []
    for b in range(blocks):
        rows = slice(b * chunk, (b + 1) * chunk)
        score, d_prob = seen[rows], back[rows]
        for j in range(chunk):
            at = b * chunk + j
            decay = jnp.where(local >= j, jnp.exp(cum[rows] - cum[at:at + 1]), 0.0)
            decay_ref[at] = decay
            reach = decay * inflow[at:at + 1]
            score = score + reach * columns(qk, rows, at)
            d_prob = d_prob + reach * columns(dm, rows, at)
        if b:
            far, near = before(b)
            got = dot_full(block_rows(b), far * inflow)
            got = [got[i * chunk:(i + 1) * chunk] for i in range(2 * heads)]
            score = score + near * by_head(got[0::2])
            d_prob = d_prob + near * by_head(got[1::2])
        scores.append(score)
        d_probs.append(d_prob)
    scores = jnp.concatenate(scores)
    d_probs = jnp.concatenate(d_probs)
    probs = jnp.exp(scores - head_reduce(scores, jnp.max))
    probs = probs / head_reduce(probs, jnp.sum)
    weighted = probs * d_probs
    d_scores = probs * (d_probs - head_reduce(weighted, jnp.sum))

    flow_ref[...] = jnp.zeros_like(flow_ref)
    for b in range(blocks):
        rows = slice(b * chunk, (b + 1) * chunk)
        mix = [jnp.zeros((chunk, steps), F32)] * heads
        pair = [jnp.zeros((chunk, steps), F32)] * heads
        if b:
            far, near = before(b)
            left = [probs[rows] * near, d_scores[rows] * near]
            left = jnp.concatenate(
                [jnp.where(mine, part, 0.0) for mine in of_head for part in (left[1], left[0])]
            )
            got = dot_full(left, far * inflow, NT)
            for h in range(heads):
                pair[h] = got[2 * h * chunk:(2 * h + 1) * chunk]
                mix[h] = got[(2 * h + 1) * chunk:(2 * h + 2) * chunk]
            flow_ref[...] += far * dot_full(block_rows(b), left, TN)
        for j in range(chunk):
            at = b * chunk + j
            decay = decay_ref[at]
            up, down_part = decay * probs[rows], decay * d_scores[rows]
            flow_ref[at:at + 1] += jnp.sum(
                up * columns(dm, rows, at) + down_part * columns(qk, rows, at),
                axis=0, keepdims=True,
            )
            up, down_part = up * inflow[at:at + 1], down_part * inflow[at:at + 1]
            for h in range(heads):
                part = slice(h * slots, (h + 1) * slots)
                here = column == at
                mix[h] = jnp.where(here, jnp.sum(up[:, part], axis=1, keepdims=True), mix[h])
                pair[h] = jnp.where(
                    here, jnp.sum(down_part[:, part], axis=1, keepdims=True), pair[h]
                )
        for h in range(heads):
            mix_ref[h, rows] = mix[h]
            pair_ref[h, rows] = pair[h]

    from_scores = d_scores * carried * scale
    from_probs = probs * carried * live
    for h in range(heads):
        part = slice(h * slots, (h + 1) * slots)
        at = slice(h * width, (h + 1) * width)
        q, og = head(q_ref, h), head(og_ref, h)
        pair = (pair_ref[h] * scale).astype(BF16)
        state_high, state_low = pieces(from_scores[:, part], 2)
        key_high, key_low = pieces(anchor_ref[0, 0, h], 2)
        d_q = dot(pair, head(k_ref, h)) + dot(state_high, key_high)
        d_q = d_q + dot(state_high, key_low) + dot(state_low, key_high)
        dq_ref[0, :, at] = d_q.astype(BF16)
        dk_ref[0, :, at] = dot(pair, q, TN).astype(BF16)
        cotangent = (og.astype(F32) * live).astype(BF16)
        dv_ref[0, :, at] = dot(mix_ref[h].astype(BF16), cotangent, TN).astype(BF16)
        ds_ref[0, 0, h] = dot(state_high, q, TN) + dot(state_low, q, TN)
        high, low = pieces(from_probs[:, part], 2)
        ds_ref[0, 1, h] = dot(high, og, TN) + dot(low, og, TN)

    flow = flow_ref[...]
    d_cum = weighted + d_scores * scores - flow * inflow
    d_keep = sum(dot(lower, part, TN) for part in pieces(d_cum, 3)) - flow * kept
    d_gates = d_keep * down * 0.125
    low = d_gates.astype(BF16)
    dx_ref[0] = dot(low, w, NT).astype(BF16)
    d_w = dot(x, low, TN)
    d_b = jnp.sum(d_gates, axis=0, keepdims=True)

    @pl.when(prompt == 0)
    def _():
        dw_ref[...] = d_w
        db_ref[...] = d_b

    @pl.when(prompt > 0)
    def _():
        dw_ref[...] += d_w
        db_ref[...] += d_b


def local_grads(x, q, k, v, og, weight, bias, anchors, lengths, advantage, interpret=False):
    prompts, steps, depth = x.shape
    inner = q.shape[2]
    lanes = weight.shape[1]
    heads = anchors.shape[2]
    chunk = 16

    def per_prompt(a):
        shape = (1,) + a.shape[1:]
        return pl.BlockSpec(shape, lambda p: (p,) + (0,) * (len(shape) - 1))

    def whole(shape):
        return pl.BlockSpec(shape, lambda p: (0,) * len(shape))

    smem = pl.BlockSpec(memory_space=pltpu.SMEM)
    shapes = (
        jax.ShapeDtypeStruct(q.shape, BF16),
        jax.ShapeDtypeStruct(q.shape, BF16),
        jax.ShapeDtypeStruct(q.shape, BF16),
        jax.ShapeDtypeStruct(x.shape, BF16),
        jax.ShapeDtypeStruct(weight.shape, F32),
        jax.ShapeDtypeStruct((1, lanes), F32),
        jax.ShapeDtypeStruct(anchors.shape, F32),
    )
    return pl.pallas_call(
        functools.partial(mix_kernel, chunk=chunk),
        grid=(prompts,),
        out_shape=shapes,
        in_specs=[smem, smem] + [per_prompt(a) for a in (x, q, k, v, og)]
        + [whole(weight.shape), whole((1, lanes)), per_prompt(anchors)],
        out_specs=tuple(per_prompt(s) for s in shapes[:4])
        + (whole(weight.shape), whole((1, lanes)), per_prompt(anchors)),
        scratch_shapes=[
            pltpu.VMEM((steps, chunk, lanes), F32),
            pltpu.VMEM((steps, lanes), F32),
            pltpu.VMEM((heads, steps, steps), F32),
            pltpu.VMEM((heads, steps, steps), F32),
        ],
        compiler_params=pltpu.CompilerParams(
            dimension_semantics=("arbitrary",), vmem_limit_bytes=48 * 2**20
        ),
        interpret=interpret,
    )(lengths, advantage, x, q, k, v, og, weight, bias.reshape(1, lanes), anchors)


class Stream:
    def __init__(self, axis, bits, source, rows, held, sems, row_axis=None, row_bits=0,
                 row_held=None, gathered=None):
        me = lax.axis_index(axis)
        self.axis, self.bits, self.source, self.rows, self.held = axis, bits, source, rows, held
        self.send_sem, self.recv_sem = sems
        self.row_axis, self.row_bits, self.row_held = row_axis, row_bits, row_held
        self.gathered = gathered
        self.mine = [me // 2 ** bit % 2 for bit in range(bits)]
        self.partner = [me + (1 - 2 * self.mine[bit]) * 2 ** bit for bit in range(bits)]
        if row_bits:
            row = lax.axis_index(row_axis)
            self.row_partner = [row + (1 - 2 * (row // 2 ** b % 2)) * 2 ** b for b in range(row_bits)]
        self.steps = bits + row_bits + (bits if gathered is not None else 0)
        self.copies = []

    def start(self, src, dst, axis, partner):
        step = len(self.copies)
        copy = pltpu.make_async_remote_copy(
            src_ref=src, dst_ref=dst, send_sem=self.send_sem.at[step],
            recv_sem=self.recv_sem.at[step], device_id={axis: partner},
            device_id_type=pl.DeviceIdType.MESH,
        )
        copy.start()
        self.copies.append(copy)

    def side(self, step, bit_value):
        free = self.bits - 1 - step
        index = (slice(None),) * free + (bit_value,)
        if step == 0:
            return self.source, index + (self.rows,)
        return self.held[step - 1], index

    def total(self):
        return self.row_held[-1] if self.row_bits else self.held[-1]

    def begin(self, step):
        if step < self.bits:
            ref, index = self.side(step, 1 - self.mine[step])
            self.start(ref.at[index], self.held[step], self.axis, self.partner[step])
            return
        step -= self.bits
        if step < self.row_bits:
            ref = self.row_held[step - 1] if step else self.held[-1]
            self.start(ref, self.row_held[step], self.row_axis, self.row_partner[step])
            return
        step -= self.row_bits
        if step == 0:
            own = tuple(self.mine[::-1]) + (self.rows,)
            self.gathered[own] = self.total()[...]
        bit = self.bits - 1 - step
        index = (slice(None),) * step + tuple(self.mine[bit::-1]) + (self.rows,)
        ref = self.gathered.at[index]
        self.start(ref, ref, self.axis, self.partner[bit])

    def end(self, step):
        self.copies[step].wait_recv()
        if step < self.bits:
            ref, index = self.side(step, self.mine[step])
            self.held[step][...] += ref[index]
        elif step < self.bits + self.row_bits:
            step -= self.bits
            ref = self.row_held[step - 1] if step else self.held[-1]
            self.row_held[step][...] += ref[...]

    def drain(self):
        for copy in self.copies:
            copy.wait_send()


def greet(axes):
    barrier = pltpu.get_barrier_semaphore()
    count = 0
    for axis, bits in axes:
        me = lax.axis_index(axis)
        for bit in range(bits):
            other = me + (1 - 2 * (me // 2 ** bit % 2)) * 2 ** bit
            pl.semaphore_signal(
                barrier, inc=1, device_id={axis: other}, device_id_type=pl.DeviceIdType.MESH
            )
            count += 1
    pl.semaphore_wait(barrier, count)


def run(streams, delays):
    last = max(s.steps + d for s, d in zip(streams, delays))
    for time in range(last + 1):
        for stream, delay in zip(streams, delays):
            step = time - delay
            if 1 <= step <= stream.steps:
                stream.end(step - 1)
            if 0 <= step < stream.steps:
                stream.begin(step)
    for stream in streams:
        stream.drain()


def halves(bits, rows, columns):
    return [
        pltpu.VMEM((2,) * (bits - 1 - step) + (rows, columns), F32) for step in range(bits)
    ]


def split_rows(rows, parts):
    each = -(-rows // parts // 8) * 8
    return [slice(at, min(at + each, rows)) for at in range(0, rows, each)]


def sum_everywhere(blocks, bits):
    rows, columns = blocks.shape[-2:]
    pieces_of = split_rows(rows, 2)
    count = len(pieces_of)

    def kernel(x_ref, o_ref, *scratch):
        streams = []
        for i, part in enumerate(pieces_of):
            own = scratch[i * (bits + 2):(i + 1) * (bits + 2)]
            streams.append(Stream("comp", bits, x_ref, part, own[:bits], own[bits:], gathered=o_ref))
        greet([("comp", bits)])
        run(streams, list(range(count)))

    scratch = []
    for part in pieces_of:
        scratch += halves(bits, part.stop - part.start, columns)
        scratch += [pltpu.SemaphoreType.DMA((2 * bits,))] * 2
    vmem = pl.BlockSpec(memory_space=pltpu.VMEM)
    return pl.pallas_call(
        kernel,
        out_shape=jax.ShapeDtypeStruct(blocks.shape, F32),
        in_specs=[vmem],
        out_specs=vmem,
        scratch_shapes=scratch,
        compiler_params=pltpu.CompilerParams(collective_id=0, has_side_effects=True),
    )(blocks)


def reduce_all(state, weight, bits, row_bits):
    rows, columns = state.shape[-2:]
    w_rows, w_columns = weight.shape[-2:]
    parts = split_rows(rows, 2)

    def kernel(s_ref, w_ref, so_ref, wo_ref, *scratch):
        w_scratch, rest = scratch[:bits + row_bits + 2], scratch[bits + row_bits + 2:]
        streams = [Stream(
            "comp", bits, w_ref, slice(None), w_scratch[:bits], w_scratch[-2:], row_axis="rows",
            row_bits=row_bits, row_held=w_scratch[bits:bits + row_bits], gathered=wo_ref,
        )]
        for i, part in enumerate(parts):
            own = rest[i * (bits + 2):(i + 1) * (bits + 2)]
            streams.append(Stream("comp", bits, s_ref, part, own[:bits], own[bits:]))
        greet([("comp", bits), ("rows", row_bits)])
        run(streams, list(range(len(streams))))
        for stream in streams[1:]:
            so_ref[stream.rows] = stream.total()[...]

    scratch = halves(bits, w_rows, w_columns)
    scratch += [pltpu.VMEM((w_rows, w_columns), F32)] * row_bits
    scratch += [pltpu.SemaphoreType.DMA((2 * bits + row_bits,))] * 2
    for part in parts:
        scratch += halves(bits, part.stop - part.start, columns)
        scratch += [pltpu.SemaphoreType.DMA((bits,))] * 2
    vmem = pl.BlockSpec(memory_space=pltpu.VMEM)
    return pl.pallas_call(
        kernel,
        out_shape=(
            jax.ShapeDtypeStruct((rows, columns), F32),
            jax.ShapeDtypeStruct(weight.shape, F32),
        ),
        in_specs=[vmem, vmem],
        out_specs=(vmem, vmem),
        scratch_shapes=scratch,
        compiler_params=pltpu.CompilerParams(collective_id=1, has_side_effects=True),
    )(state, weight)


def log2(count):
    return count.bit_length() - 1


def shards(
    comp, rows, hidden_states, queries, new_keys, new_values, out_grad, gate_weight, gate_bias,
    prompt_state, owners, lengths, advantage,
):
    bits, row_bits = log2(comp), log2(rows)
    cube = (2,) * bits
    local = prompt_state[0, 0]
    me = lax.axis_index("comp")
    mine = (owners[0] == me)[:, None, None, None, None]
    width = local.shape[-1]
    anchors = sum_everywhere(jnp.where(mine, local, 0.0).reshape(cube + (-1, width)), bits)
    dq, dk, dv, dx, d_weight, d_bias, d_state = local_grads(
        hidden_states[0, :, 0], queries[0, :, 0], new_keys[0, :, 0], new_values[0, :, 0],
        out_grad[0, :, 0], gate_weight, gate_bias, anchors.reshape(local.shape),
        lengths[0, :, 0], advantage[0, :, 0],
    )
    prompts, kinds, heads, slots, _ = local.shape
    own = slots // comp
    state = d_state.reshape(prompts * kinds * heads, comp, own, width).transpose(1, 0, 2, 3)
    lanes = gate_weight.shape[1]
    weight = jnp.concatenate(
        [d_weight.reshape(comp, -1, lanes), jnp.broadcast_to(d_bias, (comp, 8, lanes))], axis=1
    )
    state, weight = reduce_all(
        state.reshape(cube + (-1, width)), weight.reshape(cube + weight.shape[1:]), bits, row_bits
    )
    weight = weight.reshape((comp,) + weight.shape[-2:])
    return (
        dq[None, :, None], dk[None, :, None], dv[None, :, None], dx[None, :, None],
        weight[:, :-8].reshape(gate_weight.shape), weight[0, -1],
        state.reshape(1, prompts, kinds, heads, own, width),
    )


def solution(mesh):
    tokens = P("rows", None, "comp", None, None)
    return jax.shard_map(
        functools.partial(shards, mesh.shape["comp"], mesh.shape["rows"]),
        mesh=mesh,
        in_specs=(
            tokens, tokens, tokens, tokens, tokens, P(), P(),
            P("rows", "comp", None, None, None, None, None),
            P("rows", None), P("rows", None, "comp"), P("rows", None, "comp"),
        ),
        out_specs=(
            tokens, tokens, tokens, tokens, P(), P(),
            P("rows", None, None, None, "comp", None),
        ),
        check_vma=False,
    )
```

```python
import functools

import jax
import jax.numpy as jnp
from jax import lax
from jax.experimental import pallas as pl
from jax.experimental.pallas import tpu as pltpu
from jax.sharding import PartitionSpec as P

F32 = jnp.float32
BF16 = jnp.bfloat16
NN = (((1,), (0,)), ((), ()))
NT = (((1,), (1,)), ((), ()))
TN = (((0,), (0,)), ((), ()))


def dot(a, b, dims=NN):
    return lax.dot_general(a, b, dims, preferred_element_type=F32)


def dot_full(a, b, dims=NN, products=6):
    (a_axis,), (b_axis,) = dims[0]
    count = 3 if products == 6 else 2
    a, b = pieces(a, count), pieces(b, count)
    terms = [(0, 0), (0, 1), (1, 0), (1, 1), (0, 2), (2, 0)][:products][::-1]
    return dot(
        jnp.concatenate([a[i] for i, _ in terms], axis=a_axis),
        jnp.concatenate([b[j] for _, j in terms], axis=b_axis),
        dims,
    )


def pieces(x, count):
    out = []
    for _ in range(count):
        top = x.astype(BF16)
        out.append(top)
        x = x - top.astype(F32)
    return out


def mix_kernel(
    lengths_ref, advantage_ref, x_ref, q_ref, k_ref, v_ref, og_ref, w_ref, bias_ref, anchor_ref,
    dq_ref, dk_ref, dv_ref, dx_ref, dw_ref, ds_ref,
    decay_ref, mix_ref, pair_ref, *, chunk,
):
    prompt = pl.program_id(0)
    steps = x_ref.shape[1]
    heads, slots, width = anchor_ref.shape[2:]
    lanes = heads * slots
    blocks = steps // chunk
    scale = width ** (-0.5)
    lane = lax.broadcasted_iota(jnp.int32, (1, lanes), 1)
    of_head = [(lane >= h * slots) & (lane < (h + 1) * slots) for h in range(heads)]
    row = lax.broadcasted_iota(jnp.int32, (steps, 1), 0)
    column = lax.broadcasted_iota(jnp.int32, (1, steps), 1)
    lower = jnp.where(row >= column, 1.0, 0.0).astype(BF16)

    def by_head(parts):
        out = parts[-1]
        for h in range(heads - 2, -1, -1):
            out = jnp.where(lane < (h + 1) * slots, parts[h], out)
        return out

    def head_reduce(x, op):
        return by_head(
            [op(x[:, h * slots:(h + 1) * slots], axis=1, keepdims=True) for h in range(heads)]
        )

    def head(ref, h):
        return ref[0, :, h * width:(h + 1) * width]

    x = x_ref[0]
    w = w_ref[...]
    gates = dot(x, w) + bias_ref[...]
    small = jnp.exp(-jnp.abs(gates))
    one = 1.0 + small
    gap = one - 1.0
    log_one = jnp.where(gap == 0.0, small, jnp.log(one) * (small / jnp.where(gap == 0.0, 1.0, gap)))
    keep = -(jnp.maximum(-gates, 0.0) + log_one) / 8.0
    down = jnp.where(gates >= 0.0, small, 1.0) / one
    kept = jnp.exp(keep)
    series = jnp.ones_like(keep)
    for degree in range(9, 1, -1):
        series = 1.0 + keep * series * (1.0 / degree)
    inflow = jnp.where(keep > -0.5, -keep * series, 1.0 - kept)
    cum = sum(dot(lower, part) for part in pieces(keep, 3))
    carried = jnp.exp(cum)

    live = jnp.where(row < lengths_ref[prompt], advantage_ref[prompt], 0.0)
    qk, dm, seen, back = [], [], [], []
    for h in range(heads):
        q, og = head(q_ref, h), head(og_ref, h)
        qk.append(dot(q, head(k_ref, h), NT) * scale)
        dm.append(dot(og, head(v_ref, h), NT) * live)
        seen.append(sum(dot(q, part, NT) for part in pieces(anchor_ref[0, 0, h], 3)))
        back.append(sum(dot(og, part, NT) for part in pieces(anchor_ref[0, 1, h], 3)))
    seen = jnp.concatenate(seen, axis=1) * (scale * carried)
    back = jnp.concatenate(back, axis=1) * (live * carried)

    def block_rows(b):
        rows = slice(b * chunk, (b + 1) * chunk)
        return jnp.concatenate([part for h in range(heads) for part in (qk[h][rows], dm[h][rows])])

    def before(b):
        start = cum[b * chunk - 1:b * chunk]
        far = jnp.where(row < b * chunk, jnp.exp(start - cum), 0.0)
        near = jnp.exp(cum[b * chunk:(b + 1) * chunk] - start)
        return far, near

    tiles = (blocks, chunk, lanes)
    shift = chunk.bit_length() - 1
    same_block = row >> shift == column >> shift
    pair_row = lax.broadcasted_iota(jnp.int32, (heads * steps, 1), 0)
    pair_lane = lax.broadcasted_iota(jnp.int32, (1, chunk * lanes), 1)
    spread = [
        jnp.where(
            ((pair_row[:steps] & (chunk - 1)) == pair_lane >> (lanes.bit_length() - 1))
            & ((pair_lane & (lanes - 1)) >> (slots.bit_length() - 1) == h), 1.0, 0.0,
        ).astype(BF16)
        for h in range(heads)
    ]
    spread = jnp.concatenate(spread)

    def near_pairs(parts):
        kept_pairs = jnp.concatenate([jnp.where(same_block, part, 0.0) for part in parts], axis=1)
        return sum(dot(part, spread) for part in pieces(kept_pairs, 3))

    def near_sums(parts):
        got = sum(dot(part, spread, NT) for part in pieces(jnp.concatenate(parts, axis=1), 2))
        return [jnp.where(same_block, got[:, h * steps:(h + 1) * steps], 0.0) for h in range(heads)]

    def at_place(x, j):
        x = x.reshape(tiles)[:, j:j + 1]
        return jnp.broadcast_to(x, tiles).reshape(steps, lanes)

    place = row & (chunk - 1)
    qk_near, dm_near = near_pairs(qk), near_pairs(dm)
    scores, d_probs = seen, back
    for j in range(chunk):
        part = slice(j * lanes, (j + 1) * lanes)
        decay = jnp.where(place >= j, jnp.exp(cum - at_place(cum, j)), 0.0)
        decay_ref[j] = decay
        reach = decay * at_place(inflow, j)
        scores = scores + reach * qk_near[:, part]
        d_probs = d_probs + reach * dm_near[:, part]
    far_scores = [jnp.zeros((chunk, lanes), F32)]
    far_probs = [jnp.zeros((chunk, lanes), F32)]
    for b in range(1, blocks):
        far, near = before(b)
        got = dot_full(block_rows(b), far * inflow)
        got = [got[i * chunk:(i + 1) * chunk] for i in range(2 * heads)]
        far_scores.append(near * by_head(got[0::2]))
        far_probs.append(near * by_head(got[1::2]))
    scores = scores + jnp.concatenate(far_scores)
    d_probs = d_probs + jnp.concatenate(far_probs)
    probs = jnp.exp(scores - head_reduce(scores, jnp.max))
    probs = probs / head_reduce(probs, jnp.sum)
    weighted = probs * d_probs
    d_scores = probs * (d_probs - head_reduce(weighted, jnp.sum))

    flow = jnp.zeros((steps, lanes), F32)
    ups, downs = [], []
    for j in range(chunk):
        part = slice(j * lanes, (j + 1) * lanes)
        decay = decay_ref[j]
        up, away = decay * probs, decay * d_scores
        total = (up * dm_near[:, part] + away * qk_near[:, part]).reshape(tiles)
        total = jnp.broadcast_to(jnp.sum(total, axis=1, keepdims=True), tiles)
        flow = jnp.where(place == j, total.reshape(steps, lanes), flow)
        ups.append(up * at_place(inflow, j))
        downs.append(away * at_place(inflow, j))
    mix_near, pair_near = near_sums(ups), near_sums(downs)
    for h in range(heads):
        mix_ref[h] = mix_near[h]
        pair_ref[h] = pair_near[h]
    for b in range(1, blocks):
        rows = slice(b * chunk, (b + 1) * chunk)
        far, near = before(b)
        left = [d_scores[rows] * near, probs[rows] * near]
        left = jnp.concatenate(
            [jnp.where(mine, part, 0.0) for mine in of_head for part in left]
        )
        got = dot_full(left, far * inflow, NT, 3)
        for h in range(heads):
            pair_ref[h, rows] += got[2 * h * chunk:(2 * h + 1) * chunk]
            mix_ref[h, rows] += got[(2 * h + 1) * chunk:(2 * h + 2) * chunk]
        flow = flow + far * dot_full(block_rows(b), left, TN)

    from_scores = d_scores * carried * scale
    from_probs = probs * carried * live
    for h in range(heads):
        part = slice(h * slots, (h + 1) * slots)
        at = slice(h * width, (h + 1) * width)
        q, og = head(q_ref, h), head(og_ref, h)
        pair = (pair_ref[h] * scale).astype(BF16)
        state_high, state_low = pieces(from_scores[:, part], 2)
        key_high, key_low = pieces(anchor_ref[0, 0, h], 2)
        d_q = dot(pair, head(k_ref, h)) + dot(state_high, key_high)
        d_q = d_q + dot(state_high, key_low) + dot(state_low, key_high)
        dq_ref[0, :, at] = d_q.astype(BF16)
        dk_ref[0, :, at] = dot(pair, q, TN).astype(BF16)
        cotangent = (og.astype(F32) * live).astype(BF16)
        dv_ref[0, :, at] = dot(mix_ref[h].astype(BF16), cotangent, TN).astype(BF16)
        ds_ref[0, 0, h] = dot(state_high, q, TN) + dot(state_low, q, TN)
        high, low = pieces(from_probs[:, part], 2)
        ds_ref[0, 1, h] = dot(high, og, TN) + dot(low, og, TN)

    d_cum = weighted + d_scores * scores - flow * inflow
    d_keep = sum(dot(lower, part, TN) for part in pieces(d_cum, 3)) - flow * kept
    d_gates = d_keep * down * 0.125
    low = d_gates.astype(BF16)
    dx_ref[0] = dot(low, w, NT).astype(BF16)
    d_w = dot(x, low, TN)
    d_b = jnp.sum(d_gates, axis=0, keepdims=True)

    d_b = jnp.broadcast_to(d_b, (8, lanes))
    count = dw_ref.shape[1] - 8

    @pl.when(prompt == 0)
    def _():
        dw_ref[...] = jnp.zeros_like(dw_ref)

    for c in range(dw_ref.shape[0]):
        dw_ref[c, :count] += d_w[c * count:(c + 1) * count]
        dw_ref[c, count:] += d_b


def local_grads(comp, x, q, k, v, og, weight, bias, anchors, lengths, advantage, chunk=8, interpret=False):
    prompts, steps, depth = x.shape
    inner = q.shape[2]
    lanes = weight.shape[1]
    heads = anchors.shape[2]
    gate_shape = (comp, depth // comp + 8, lanes)

    def per_prompt(a):
        shape = (1,) + a.shape[1:]
        return pl.BlockSpec(shape, lambda p: (p,) + (0,) * (len(shape) - 1))

    def whole(shape):
        return pl.BlockSpec(shape, lambda p: (0,) * len(shape))

    smem = pl.BlockSpec(memory_space=pltpu.SMEM)
    shapes = (
        jax.ShapeDtypeStruct(q.shape, BF16),
        jax.ShapeDtypeStruct(q.shape, BF16),
        jax.ShapeDtypeStruct(q.shape, BF16),
        jax.ShapeDtypeStruct(x.shape, BF16),
        jax.ShapeDtypeStruct(gate_shape, F32),
        jax.ShapeDtypeStruct(anchors.shape, F32),
    )
    return pl.pallas_call(
        functools.partial(mix_kernel, chunk=chunk),
        grid=(prompts,),
        out_shape=shapes,
        in_specs=[smem, smem] + [per_prompt(a) for a in (x, q, k, v, og)]
        + [whole(weight.shape), whole((1, lanes)), per_prompt(anchors)],
        out_specs=tuple(per_prompt(s) for s in shapes[:4])
        + (whole(gate_shape), per_prompt(anchors)),
        scratch_shapes=[
            pltpu.VMEM((chunk, steps, lanes), F32),
            pltpu.VMEM((heads, steps, steps), F32),
            pltpu.VMEM((heads, steps, steps), F32),
        ],
        compiler_params=pltpu.CompilerParams(
            dimension_semantics=("arbitrary",), vmem_limit_bytes=48 * 2**20
        ),
        interpret=interpret,
    )(lengths, advantage, x, q, k, v, og, weight, bias.reshape(1, lanes), anchors)


class Stream:
    def __init__(self, axis, bits, source, rows, held, sems, row_axis=None, row_bits=0,
                 row_held=None, gathered=None):
        me = lax.axis_index(axis)
        self.axis, self.bits, self.source, self.rows, self.held = axis, bits, source, rows, held
        self.send_sem, self.recv_sem = sems
        self.row_axis, self.row_bits, self.row_held = row_axis, row_bits, row_held
        self.gathered = gathered
        self.mine = [me // 2 ** bit % 2 for bit in range(bits)]
        self.partner = [me + (1 - 2 * self.mine[bit]) * 2 ** bit for bit in range(bits)]
        if row_bits:
            row = lax.axis_index(row_axis)
            self.row_partner = [row + (1 - 2 * (row // 2 ** b % 2)) * 2 ** b for b in range(row_bits)]
        self.steps = bits + row_bits + (bits if gathered is not None else 0)
        self.copies = []

    def start(self, src, dst, axis, partner):
        step = len(self.copies)
        copy = pltpu.make_async_remote_copy(
            src_ref=src, dst_ref=dst, send_sem=self.send_sem.at[step],
            recv_sem=self.recv_sem.at[step], device_id={axis: partner},
            device_id_type=pl.DeviceIdType.MESH,
        )
        copy.start()
        self.copies.append(copy)

    def side(self, step, bit_value):
        free = self.bits - 1 - step
        index = (slice(None),) * free + (bit_value,)
        if step == 0:
            return self.source, index + (self.rows,)
        return self.held[step - 1], index

    def total(self):
        return self.row_held[-1] if self.row_bits else self.held[-1]

    def begin(self, step):
        if step < self.bits:
            ref, index = self.side(step, 1 - self.mine[step])
            self.start(ref.at[index], self.held[step], self.axis, self.partner[step])
            return
        step -= self.bits
        if step < self.row_bits:
            ref = self.row_held[step - 1] if step else self.held[-1]
            self.start(ref, self.row_held[step], self.row_axis, self.row_partner[step])
            return
        step -= self.row_bits
        if step == 0:
            own = tuple(self.mine[::-1]) + (self.rows,)
            self.gathered[own] = self.total()[...]
        bit = self.bits - 1 - step
        index = (slice(None),) * step + tuple(self.mine[bit::-1]) + (self.rows,)
        ref = self.gathered.at[index]
        self.start(ref, ref, self.axis, self.partner[bit])

    def end(self, step):
        self.copies[step].wait_recv()
        if step < self.bits:
            ref, index = self.side(step, self.mine[step])
            self.held[step][...] += ref[index]
        elif step < self.bits + self.row_bits:
            step -= self.bits
            ref = self.row_held[step - 1] if step else self.held[-1]
            self.row_held[step][...] += ref[...]

    def drain(self):
        for copy in self.copies:
            copy.wait_send()


def greet(axes):
    barrier = pltpu.get_barrier_semaphore()
    count = 0
    for axis, bits in axes:
        me = lax.axis_index(axis)
        for bit in range(bits):
            other = me + (1 - 2 * (me // 2 ** bit % 2)) * 2 ** bit
            pl.semaphore_signal(
                barrier, inc=1, device_id={axis: other}, device_id_type=pl.DeviceIdType.MESH
            )
            count += 1
    pl.semaphore_wait(barrier, count)


def run(streams, delays):
    last = max(s.steps + d for s, d in zip(streams, delays))
    for time in range(last + 1):
        for stream, delay in zip(streams, delays):
            step = time - delay
            if 1 <= step <= stream.steps:
                stream.end(step - 1)
            if 0 <= step < stream.steps:
                stream.begin(step)
    for stream in streams:
        stream.drain()


def halves(bits, rows, columns):
    return [
        pltpu.VMEM((2,) * (bits - 1 - step) + (rows, columns), F32) for step in range(bits)
    ]


def split_rows(rows, parts):
    each = -(-rows // parts // 8) * 8
    return [slice(at, min(at + each, rows)) for at in range(0, rows, each)]


def sum_everywhere(blocks, bits):
    rows, columns = blocks.shape[-2:]
    pieces_of = split_rows(rows, 4)
    count = len(pieces_of)

    def kernel(x_ref, o_ref, *scratch):
        streams = []
        for i, part in enumerate(pieces_of):
            own = scratch[i * (bits + 2):(i + 1) * (bits + 2)]
            streams.append(Stream("comp", bits, x_ref, part, own[:bits], own[bits:], gathered=o_ref))
        greet([("comp", bits)])
        run(streams, list(range(count)))

    scratch = []
    for part in pieces_of:
        scratch += halves(bits, part.stop - part.start, columns)
        scratch += [pltpu.SemaphoreType.DMA((2 * bits,))] * 2
    vmem = pl.BlockSpec(memory_space=pltpu.VMEM)
    return pl.pallas_call(
        kernel,
        out_shape=jax.ShapeDtypeStruct(blocks.shape, F32),
        in_specs=[vmem],
        out_specs=vmem,
        scratch_shapes=scratch,
        compiler_params=pltpu.CompilerParams(collective_id=0, has_side_effects=True),
    )(blocks)


def reduce_all(state, weight, bits, row_bits):
    rows, columns = state.shape[-2:]
    w_rows, w_columns = weight.shape[-2:]
    parts = split_rows(rows, 4)
    w_parts = split_rows(w_rows, 2)

    def kernel(s_ref, w_ref, so_ref, wo_ref, *scratch):
        streams = []
        for part in w_parts:
            own, scratch = scratch[:bits + row_bits + 2], scratch[bits + row_bits + 2:]
            streams.append(Stream(
                "comp", bits, w_ref, part, own[:bits], own[-2:], row_axis="rows",
                row_bits=row_bits, row_held=own[bits:bits + row_bits], gathered=wo_ref,
            ))
        for part in parts:
            own, scratch = scratch[:bits + 2], scratch[bits + 2:]
            streams.append(Stream("comp", bits, s_ref, part, own[:bits], own[bits:]))
        greet([("comp", bits), ("rows", row_bits)])
        run(streams, list(range(len(streams))))
        for stream in streams[len(w_parts):]:
            so_ref[stream.rows] = stream.total()[...]

    scratch = []
    for part in w_parts:
        scratch += halves(bits, part.stop - part.start, w_columns)
        scratch += [pltpu.VMEM((part.stop - part.start, w_columns), F32)] * row_bits
        scratch += [pltpu.SemaphoreType.DMA((2 * bits + row_bits,))] * 2
    for part in parts:
        scratch += halves(bits, part.stop - part.start, columns)
        scratch += [pltpu.SemaphoreType.DMA((bits,))] * 2
    vmem = pl.BlockSpec(memory_space=pltpu.VMEM)
    return pl.pallas_call(
        kernel,
        out_shape=(
            jax.ShapeDtypeStruct((rows, columns), F32),
            jax.ShapeDtypeStruct(weight.shape, F32),
        ),
        in_specs=[vmem, vmem],
        out_specs=(vmem, vmem),
        scratch_shapes=scratch,
        compiler_params=pltpu.CompilerParams(collective_id=1, has_side_effects=True),
    )(state, weight)


def log2(count):
    return count.bit_length() - 1


def shards(
    comp, rows, hidden_states, queries, new_keys, new_values, out_grad, gate_weight, gate_bias,
    prompt_state, owners, lengths, advantage,
):
    bits, row_bits = log2(comp), log2(rows)
    cube = (2,) * bits
    local = prompt_state[0, 0]
    me = lax.axis_index("comp")
    mine = (owners[0] == me)[:, None, None, None, None]
    width = local.shape[-1]
    anchors = sum_everywhere(jnp.where(mine, local, 0.0).reshape(cube + (-1, width)), bits)
    dq, dk, dv, dx, weight, d_state = local_grads(
        comp, hidden_states[0, :, 0], queries[0, :, 0], new_keys[0, :, 0], new_values[0, :, 0],
        out_grad[0, :, 0], gate_weight, gate_bias, anchors.reshape(local.shape),
        lengths[0, :, 0], advantage[0, :, 0],
    )
    prompts, kinds, heads, slots, _ = local.shape
    own = slots // comp
    state = d_state.reshape(prompts * kinds * heads, comp, own, width).transpose(1, 0, 2, 3)
    state, weight = reduce_all(
        state.reshape(cube + (-1, width)), weight.reshape(cube + weight.shape[1:]), bits, row_bits
    )
    weight = weight.reshape((comp,) + weight.shape[-2:])
    return (
        dq[None, :, None], dk[None, :, None], dv[None, :, None], dx[None, :, None],
        weight[:, :-8].reshape(gate_weight.shape), weight[0, -1],
        state.reshape(1, prompts, kinds, heads, own, width),
    )


def solution(mesh):
    tokens = P("rows", None, "comp", None, None)
    return jax.shard_map(
        functools.partial(shards, mesh.shape["comp"], mesh.shape["rows"]),
        mesh=mesh,
        in_specs=(
            tokens, tokens, tokens, tokens, tokens, P(), P(),
            P("rows", "comp", None, None, None, None, None),
            P("rows", None), P("rows", None, "comp"), P("rows", None, "comp"),
        ),
        out_specs=(
            tokens, tokens, tokens, tokens, P(), P(),
            P("rows", None, None, None, "comp", None),
        ),
        check_vma=False,
    )
```

```python
import functools

import jax
import jax.numpy as jnp
from jax import lax
from jax.experimental import pallas as pl
from jax.experimental.pallas import tpu as pltpu
from jax.sharding import PartitionSpec as P

F32 = jnp.float32
BF16 = jnp.bfloat16
NN = (((1,), (0,)), ((), ()))
NT = (((1,), (1,)), ((), ()))
TN = (((0,), (0,)), ((), ()))


def dot(a, b, dims=NN):
    return lax.dot_general(a, b, dims, preferred_element_type=F32)


def dot_full(a, b, dims=NN, products=6):
    (a_axis,), (b_axis,) = dims[0]
    count = 3 if products == 6 else 2
    a, b = pieces(a, count), pieces(b, count)
    terms = [(0, 0), (0, 1), (1, 0), (1, 1), (0, 2), (2, 0)][:products][::-1]
    return dot(
        jnp.concatenate([a[i] for i, _ in terms], axis=a_axis),
        jnp.concatenate([b[j] for _, j in terms], axis=b_axis),
        dims,
    )


def pieces(x, count):
    out = []
    for _ in range(count):
        top = x.astype(BF16)
        out.append(top)
        x = x - top.astype(F32)
    return out


def mix_kernel(
    lengths_ref, advantage_ref, x_ref, q_ref, k_ref, v_ref, og_ref, w_ref, bias_ref, anchor_ref,
    dq_ref, dk_ref, dv_ref, dx_ref, dw_ref, ds_ref,
    decay_ref, mix_ref, pair_ref, *, chunk,
):
    prompt = pl.program_id(0)
    steps = x_ref.shape[1]
    heads, slots, width = anchor_ref.shape[2:]
    lanes = heads * slots
    blocks = steps // chunk
    scale = width ** (-0.5)
    lane = lax.broadcasted_iota(jnp.int32, (1, lanes), 1)
    of_head = [(lane >= h * slots) & (lane < (h + 1) * slots) for h in range(heads)]
    row = lax.broadcasted_iota(jnp.int32, (steps, 1), 0)
    column = lax.broadcasted_iota(jnp.int32, (1, steps), 1)
    lower = jnp.where(row >= column, 1.0, 0.0).astype(BF16)

    def by_head(parts):
        out = parts[-1]
        for h in range(heads - 2, -1, -1):
            out = jnp.where(lane < (h + 1) * slots, parts[h], out)
        return out

    def head_reduce(x, op):
        return by_head(
            [op(x[:, h * slots:(h + 1) * slots], axis=1, keepdims=True) for h in range(heads)]
        )

    def head(ref, h):
        return ref[0, :, h * width:(h + 1) * width]

    x = x_ref[0]
    w = w_ref[...]
    gates = dot(x, w) + bias_ref[...]
    small = jnp.exp(-jnp.abs(gates))
    one = 1.0 + small
    gap = one - 1.0
    log_one = jnp.where(gap == 0.0, small, jnp.log(one) * (small / jnp.where(gap == 0.0, 1.0, gap)))
    keep = -(jnp.maximum(-gates, 0.0) + log_one) / 8.0
    down = jnp.where(gates >= 0.0, small, 1.0) / one
    kept = jnp.exp(keep)
    series = jnp.ones_like(keep)
    for degree in range(9, 1, -1):
        series = 1.0 + keep * series * (1.0 / degree)
    inflow = jnp.where(keep > -0.5, -keep * series, 1.0 - kept)
    cum = sum(dot(lower, part) for part in pieces(keep, 3))
    carried = jnp.exp(cum)

    live = jnp.where(row < lengths_ref[prompt], advantage_ref[prompt], 0.0)
    qk, dm, seen, back = [], [], [], []
    for h in range(heads):
        q, og = head(q_ref, h), head(og_ref, h)
        qk.append(dot(q, head(k_ref, h), NT) * scale)
        dm.append(dot(og, head(v_ref, h), NT) * live)
        seen.append(sum(dot(q, part, NT) for part in pieces(anchor_ref[0, 0, h], 3)))
        back.append(sum(dot(og, part, NT) for part in pieces(anchor_ref[0, 1, h], 3)))
    seen = jnp.concatenate(seen, axis=1) * (scale * carried)
    back = jnp.concatenate(back, axis=1) * (live * carried)

    def block_rows(b):
        rows = slice(b * chunk, (b + 1) * chunk)
        return jnp.concatenate([part for h in range(heads) for part in (qk[h][rows], dm[h][rows])])

    def before(b):
        start = cum[b * chunk - 1:b * chunk]
        far = jnp.where(row < b * chunk, jnp.exp(start - cum), 0.0)
        near = jnp.exp(cum[b * chunk:(b + 1) * chunk] - start)
        return far, near

    tiles = (blocks, chunk, lanes)
    shift = chunk.bit_length() - 1
    same_block = row >> shift == column >> shift
    pair_row = lax.broadcasted_iota(jnp.int32, (heads * steps, 1), 0)
    pair_lane = lax.broadcasted_iota(jnp.int32, (1, chunk * lanes), 1)
    spread = [
        jnp.where(
            ((pair_row[:steps] & (chunk - 1)) == pair_lane >> (lanes.bit_length() - 1))
            & ((pair_lane & (lanes - 1)) >> (slots.bit_length() - 1) == h), 1.0, 0.0,
        ).astype(BF16)
        for h in range(heads)
    ]
    spread = jnp.concatenate(spread)

    def near_pairs(parts):
        kept_pairs = jnp.concatenate([jnp.where(same_block, part, 0.0) for part in parts], axis=1)
        return sum(dot(part, spread) for part in pieces(kept_pairs, 3))

    def near_sums(parts):
        got = sum(dot(part, spread, NT) for part in pieces(jnp.concatenate(parts, axis=1), 2))
        return [jnp.where(same_block, got[:, h * steps:(h + 1) * steps], 0.0) for h in range(heads)]

    def at_place(x, j):
        x = x.reshape(tiles)[:, j:j + 1]
        return jnp.broadcast_to(x, tiles).reshape(steps, lanes)

    place = row & (chunk - 1)
    qk_near, dm_near = near_pairs(qk), near_pairs(dm)
    scores, d_probs = seen, back
    for j in range(chunk):
        part = slice(j * lanes, (j + 1) * lanes)
        decay = jnp.where(place >= j, jnp.exp(cum - at_place(cum, j)), 0.0)
        decay_ref[j] = decay
        reach = decay * at_place(inflow, j)
        scores = scores + reach * qk_near[:, part]
        d_probs = d_probs + reach * dm_near[:, part]
    far_scores = [jnp.zeros((chunk, lanes), F32)]
    far_probs = [jnp.zeros((chunk, lanes), F32)]
    for b in range(1, blocks):
        far, near = before(b)
        got = dot_full(block_rows(b), far * inflow)
        got = [got[i * chunk:(i + 1) * chunk] for i in range(2 * heads)]
        far_scores.append(near * by_head(got[0::2]))
        far_probs.append(near * by_head(got[1::2]))
    scores = scores + jnp.concatenate(far_scores)
    d_probs = d_probs + jnp.concatenate(far_probs)
    probs = jnp.exp(scores - head_reduce(scores, jnp.max))
    probs = probs / head_reduce(probs, jnp.sum)
    weighted = probs * d_probs
    d_scores = probs * (d_probs - head_reduce(weighted, jnp.sum))

    flow = jnp.zeros((steps, lanes), F32)
    ups, downs = [], []
    for j in range(chunk):
        part = slice(j * lanes, (j + 1) * lanes)
        decay = decay_ref[j]
        up, away = decay * probs, decay * d_scores
        total = (up * dm_near[:, part] + away * qk_near[:, part]).reshape(tiles)
        total = jnp.broadcast_to(jnp.sum(total, axis=1, keepdims=True), tiles)
        flow = jnp.where(place == j, total.reshape(steps, lanes), flow)
        ups.append(up * at_place(inflow, j))
        downs.append(away * at_place(inflow, j))
    mix_near, pair_near = near_sums(ups), near_sums(downs)
    for h in range(heads):
        mix_ref[h] = mix_near[h]
        pair_ref[h] = pair_near[h]
    for b in range(1, blocks):
        rows = slice(b * chunk, (b + 1) * chunk)
        far, near = before(b)
        left = [d_scores[rows] * near, probs[rows] * near]
        left = jnp.concatenate(
            [jnp.where(mine, part, 0.0) for mine in of_head for part in left]
        )
        got = dot_full(left, far * inflow, NT, 3)
        for h in range(heads):
            pair_ref[h, rows] += got[2 * h * chunk:(2 * h + 1) * chunk]
            mix_ref[h, rows] += got[(2 * h + 1) * chunk:(2 * h + 2) * chunk]
        flow = flow + far * dot_full(block_rows(b), left, TN)

    from_scores = d_scores * carried * scale
    from_probs = probs * carried * live
    for h in range(heads):
        part = slice(h * slots, (h + 1) * slots)
        at = slice(h * width, (h + 1) * width)
        q, og = head(q_ref, h), head(og_ref, h)
        pair = (pair_ref[h] * scale).astype(BF16)
        state_high, state_low = pieces(from_scores[:, part], 2)
        key_high, key_low = pieces(anchor_ref[0, 0, h], 2)
        d_q = dot(pair, head(k_ref, h)) + dot(state_high, key_high)
        d_q = d_q + dot(state_high, key_low) + dot(state_low, key_high)
        dq_ref[0, :, at] = d_q.astype(BF16)
        dk_ref[0, :, at] = dot(pair, q, TN).astype(BF16)
        cotangent = (og.astype(F32) * live).astype(BF16)
        dv_ref[0, :, at] = dot(mix_ref[h].astype(BF16), cotangent, TN).astype(BF16)
        ds_ref[0, 0, h] = dot(state_high, q, TN) + dot(state_low, q, TN)
        high, low = pieces(from_probs[:, part], 2)
        ds_ref[0, 1, h] = dot(high, og, TN) + dot(low, og, TN)

    d_cum = weighted + d_scores * scores - flow * inflow
    d_keep = sum(dot(lower, part, TN) for part in pieces(d_cum, 3)) - flow * kept
    d_gates = d_keep * down * 0.125
    low = d_gates.astype(BF16)
    dx_ref[0] = dot(low, w, NT).astype(BF16)
    d_w = dot(x, low, TN)
    d_b = jnp.sum(d_gates, axis=0, keepdims=True)

    d_b = jnp.broadcast_to(d_b, (8, lanes))
    count = dw_ref.shape[1] - 8

    @pl.when(prompt == 0)
    def _():
        dw_ref[...] = jnp.zeros_like(dw_ref)

    for c in range(dw_ref.shape[0]):
        dw_ref[c, :count] += d_w[c * count:(c + 1) * count]
        dw_ref[c, count:] += d_b


def local_grads(comp, x, q, k, v, og, weight, bias, anchors, lengths, advantage, chunk=8, interpret=False):
    prompts, steps, depth = x.shape
    inner = q.shape[2]
    lanes = weight.shape[1]
    heads = anchors.shape[2]
    gate_shape = (comp, depth // comp + 8, lanes)

    def per_prompt(a):
        shape = (1,) + a.shape[1:]
        return pl.BlockSpec(shape, lambda p: (p,) + (0,) * (len(shape) - 1))

    def whole(shape):
        return pl.BlockSpec(shape, lambda p: (0,) * len(shape))

    smem = pl.BlockSpec(memory_space=pltpu.SMEM)
    shapes = (
        jax.ShapeDtypeStruct(q.shape, BF16),
        jax.ShapeDtypeStruct(q.shape, BF16),
        jax.ShapeDtypeStruct(q.shape, BF16),
        jax.ShapeDtypeStruct(x.shape, BF16),
        jax.ShapeDtypeStruct(gate_shape, F32),
        jax.ShapeDtypeStruct(anchors.shape, F32),
    )
    return pl.pallas_call(
        functools.partial(mix_kernel, chunk=chunk),
        grid=(prompts,),
        out_shape=shapes,
        in_specs=[smem, smem] + [per_prompt(a) for a in (x, q, k, v, og)]
        + [whole(weight.shape), whole((1, lanes)), per_prompt(anchors)],
        out_specs=tuple(per_prompt(s) for s in shapes[:4])
        + (whole(gate_shape), per_prompt(anchors)),
        scratch_shapes=[
            pltpu.VMEM((chunk, steps, lanes), F32),
            pltpu.VMEM((heads, steps, steps), F32),
            pltpu.VMEM((heads, steps, steps), F32),
        ],
        compiler_params=pltpu.CompilerParams(
            dimension_semantics=("arbitrary",), vmem_limit_bytes=48 * 2**20
        ),
        interpret=interpret,
    )(lengths, advantage, x, q, k, v, og, weight, bias.reshape(1, lanes), anchors)


class Stream:
    def __init__(self, axis, bits, source, rows, held, sems, row_axis=None, row_bits=0,
                 row_held=None, gathered=None):
        me = lax.axis_index(axis)
        self.axis, self.bits, self.source, self.rows, self.held = axis, bits, source, rows, held
        self.send_sem, self.recv_sem = sems
        self.row_axis, self.row_bits, self.row_held = row_axis, row_bits, row_held
        self.gathered = gathered
        self.mine = [me // 2 ** bit % 2 for bit in range(bits)]
        self.partner = [me + (1 - 2 * self.mine[bit]) * 2 ** bit for bit in range(bits)]
        if row_bits:
            row = lax.axis_index(row_axis)
            self.row_partner = [row + (1 - 2 * (row // 2 ** b % 2)) * 2 ** b for b in range(row_bits)]
        self.steps = bits + row_bits + (bits if gathered is not None else 0)
        self.copies = []

    def start(self, src, dst, axis, partner):
        step = len(self.copies)
        copy = pltpu.make_async_remote_copy(
            src_ref=src, dst_ref=dst, send_sem=self.send_sem.at[step],
            recv_sem=self.recv_sem.at[step], device_id={axis: partner},
            device_id_type=pl.DeviceIdType.MESH,
        )
        copy.start()
        self.copies.append(copy)

    def side(self, step, bit_value):
        free = self.bits - 1 - step
        index = (slice(None),) * free + (bit_value,)
        if step == 0:
            return self.source, index + (self.rows,)
        return self.held[step - 1], index

    def total(self):
        return self.row_held[-1] if self.row_bits else self.held[-1]

    def begin(self, step):
        if step < self.bits:
            ref, index = self.side(step, 1 - self.mine[step])
            self.start(ref.at[index], self.held[step], self.axis, self.partner[step])
            return
        step -= self.bits
        if step < self.row_bits:
            ref = self.row_held[step - 1] if step else self.held[-1]
            self.start(ref, self.row_held[step], self.row_axis, self.row_partner[step])
            return
        step -= self.row_bits
        if step == 0:
            own = tuple(self.mine[::-1]) + (self.rows,)
            self.gathered[own] = self.total()[...]
        bit = self.bits - 1 - step
        index = (slice(None),) * step + tuple(self.mine[bit::-1]) + (self.rows,)
        ref = self.gathered.at[index]
        self.start(ref, ref, self.axis, self.partner[bit])

    def end(self, step):
        self.copies[step].wait_recv()
        if step < self.bits:
            ref, index = self.side(step, self.mine[step])
            self.held[step][...] += ref[index]
        elif step < self.bits + self.row_bits:
            step -= self.bits
            ref = self.row_held[step - 1] if step else self.held[-1]
            self.row_held[step][...] += ref[...]

    def drain(self):
        for copy in self.copies:
            copy.wait_send()


def greet(axes):
    barrier = pltpu.get_barrier_semaphore()
    count = 0
    for axis, bits in axes:
        me = lax.axis_index(axis)
        for bit in range(bits):
            other = me + (1 - 2 * (me // 2 ** bit % 2)) * 2 ** bit
            pl.semaphore_signal(
                barrier, inc=1, device_id={axis: other}, device_id_type=pl.DeviceIdType.MESH
            )
            count += 1
    pl.semaphore_wait(barrier, count)


def run(streams, delays):
    last = max(s.steps + d for s, d in zip(streams, delays))
    for time in range(last + 1):
        for stream, delay in zip(streams, delays):
            step = time - delay
            if 1 <= step <= stream.steps:
                stream.end(step - 1)
            if 0 <= step < stream.steps:
                stream.begin(step)
    for stream in streams:
        stream.drain()


def halves(bits, rows, columns):
    return [
        pltpu.VMEM((2,) * (bits - 1 - step) + (rows, columns), F32) for step in range(bits)
    ]


def split_rows(rows, parts):
    each = -(-rows // parts // 8) * 8
    return [slice(at, min(at + each, rows)) for at in range(0, rows, each)]


def sum_everywhere(blocks, bits):
    rows, columns = blocks.shape[-2:]
    pieces_of = split_rows(rows, 2)
    count = len(pieces_of)

    def kernel(x_ref, o_ref, *scratch):
        streams = []
        for i, part in enumerate(pieces_of):
            own = scratch[i * (bits + 2):(i + 1) * (bits + 2)]
            streams.append(Stream("comp", bits, x_ref, part, own[:bits], own[bits:], gathered=o_ref))
        greet([("comp", bits)])
        run(streams, list(range(count)))

    scratch = []
    for part in pieces_of:
        scratch += halves(bits, part.stop - part.start, columns)
        scratch += [pltpu.SemaphoreType.DMA((2 * bits,))] * 2
    vmem = pl.BlockSpec(memory_space=pltpu.VMEM)
    return pl.pallas_call(
        kernel,
        out_shape=jax.ShapeDtypeStruct(blocks.shape, F32),
        in_specs=[vmem],
        out_specs=vmem,
        scratch_shapes=scratch,
        compiler_params=pltpu.CompilerParams(collective_id=0, has_side_effects=True),
    )(blocks)


def reduce_all(state, weight, bits, row_bits):
    rows, columns = state.shape[-2:]
    w_rows, w_columns = weight.shape[-2:]
    parts = split_rows(rows, 4)
    w_parts = split_rows(w_rows, 2)

    def kernel(s_ref, w_ref, so_ref, wo_ref, *scratch):
        streams = []
        for part in w_parts:
            own, scratch = scratch[:bits + row_bits + 2], scratch[bits + row_bits + 2:]
            streams.append(Stream(
                "comp", bits, w_ref, part, own[:bits], own[-2:], row_axis="rows",
                row_bits=row_bits, row_held=own[bits:bits + row_bits], gathered=wo_ref,
            ))
        for part in parts:
            own, scratch = scratch[:bits + 2], scratch[bits + 2:]
            streams.append(Stream("comp", bits, s_ref, part, own[:bits], own[bits:]))
        greet([("comp", bits), ("rows", row_bits)])
        run(streams, list(range(len(streams))))
        for stream in streams[len(w_parts):]:
            so_ref[stream.rows] = stream.total()[...]

    scratch = []
    for part in w_parts:
        scratch += halves(bits, part.stop - part.start, w_columns)
        scratch += [pltpu.VMEM((part.stop - part.start, w_columns), F32)] * row_bits
        scratch += [pltpu.SemaphoreType.DMA((2 * bits + row_bits,))] * 2
    for part in parts:
        scratch += halves(bits, part.stop - part.start, columns)
        scratch += [pltpu.SemaphoreType.DMA((bits,))] * 2
    vmem = pl.BlockSpec(memory_space=pltpu.VMEM)
    return pl.pallas_call(
        kernel,
        out_shape=(
            jax.ShapeDtypeStruct((rows, columns), F32),
            jax.ShapeDtypeStruct(weight.shape, F32),
        ),
        in_specs=[vmem, vmem],
        out_specs=(vmem, vmem),
        scratch_shapes=scratch,
        compiler_params=pltpu.CompilerParams(collective_id=1, has_side_effects=True),
    )(state, weight)


def log2(count):
    return count.bit_length() - 1


def shards(
    comp, rows, hidden_states, queries, new_keys, new_values, out_grad, gate_weight, gate_bias,
    prompt_state, owners, lengths, advantage,
):
    bits, row_bits = log2(comp), log2(rows)
    cube = (2,) * bits
    local = prompt_state[0, 0]
    me = lax.axis_index("comp")
    mine = (owners[0] == me)[:, None, None, None, None]
    width = local.shape[-1]
    anchors = sum_everywhere(jnp.where(mine, local, 0.0).reshape(cube + (-1, width)), bits)
    dq, dk, dv, dx, weight, d_state = local_grads(
        comp, hidden_states[0, :, 0], queries[0, :, 0], new_keys[0, :, 0], new_values[0, :, 0],
        out_grad[0, :, 0], gate_weight, gate_bias, anchors.reshape(local.shape),
        lengths[0, :, 0], advantage[0, :, 0],
    )
    prompts, kinds, heads, slots, _ = local.shape
    own = slots // comp
    state = d_state.reshape(prompts * kinds * heads, comp, own, width).transpose(1, 0, 2, 3)
    state, weight = reduce_all(
        state.reshape(cube + (-1, width)), weight.reshape(cube + weight.shape[1:]), bits, row_bits
    )
    weight = weight.reshape((comp,) + weight.shape[-2:])
    return (
        dq[None, :, None], dk[None, :, None], dv[None, :, None], dx[None, :, None],
        weight[:, :-8].reshape(gate_weight.shape), weight[0, -1],
        state.reshape(1, prompts, kinds, heads, own, width),
    )


def solution(mesh):
    tokens = P("rows", None, "comp", None, None)
    return jax.shard_map(
        functools.partial(shards, mesh.shape["comp"], mesh.shape["rows"]),
        mesh=mesh,
        in_specs=(
            tokens, tokens, tokens, tokens, tokens, P(), P(),
            P("rows", "comp", None, None, None, None, None),
            P("rows", None), P("rows", None, "comp"), P("rows", None, "comp"),
        ),
        out_specs=(
            tokens, tokens, tokens, tokens, P(), P(),
            P("rows", None, None, None, "comp", None),
        ),
        check_vma=False,
    )
```
